32 devices in a mesh: groups: 2 (over y), tm: 4 (over z), rows: 4 (over x, core).
Axes of the slice: x: 2, y: 2, z: 4, core: 2. Of those that a mesh axis runs over, the one named last changes fastest.
Arguments:
- latents: bfloat16 [16, 16, 128, 256], P(('groups', 'tm'), 'rows'), parts along dimension 0, may hold values from -6 to 6
- weight_in: bfloat16 [3, 3, 256, 256], replicated, may hold values from -0.125 to 0.125
- weight_out: bfloat16 [3, 3, 256, 256], replicated, may hold values from -0.0234375 to 0.0234375
- decay_table: float32 [16], replicated, may hold values from 0.99 to 0.999
- decay_index: int32 [256], replicated, may hold values from 0 to 15
Outputs:
- updated: bfloat16 [16, 16, 128, 256], P(('groups', 'tm'), 'rows'), parts along dimension 0
The draws below stay inside these ranges and needn't reach their ends.
There are 2 independent parts, one for each index of `groups`. The reference program is written for one: setup_inputs(seed, part) draws one part's arguments, and reference() takes and returns one part's arrays. A program takes and returns all parts, laid end to end along the dimension named above; an argument that names none is the same for every part. Nothing has to cross between parts.
All inputs are finite; a program needn't handle non-finite values.
Results may differ from the reference program's by a relative error of at most 0.0032.
Values may be sent and summed in bfloat16 or wider, within the bound.
A program may use at most 64 MiB of HBM per device.

```python
import jax
import jax.numpy as jnp
from jax import lax

C = 256
W = 128
LEVELS = 16
FRAMES = 8
H = 16


def place_ends(drawn, stream_key, smallest, largest):
    longest = drawn.shape.index(max(drawn.shape))
    spots = []
    for shift in (0, 1):
        where = [jax.random.randint(jax.random.fold_in(stream_key, axis), (), 0, length) for axis, length in enumerate(drawn.shape)]
        where[longest] = (where[longest] + shift) % drawn.shape[longest]
        spots.append(tuple(where))
    return drawn.at[spots[0]].set(smallest).at[spots[1]].set(largest)


def block_levels(key, extent, pieces, low, largest):
    gain = 1.0
    for position, shards_of in pieces:
        draws = jax.random.uniform(jax.random.fold_in(jax.random.fold_in(key, 6), position), (shards_of,), jnp.float32, low / len(pieces), largest / len(pieces))
        gain = gain * jnp.repeat(jnp.exp(draws), extent[position] // shards_of).reshape((-1,) + (1,) * (len(extent) - 1 - position))
    return gain


def centred(stream_key, shape, scale, most, shards=(), dtype=jnp.bfloat16):
    gain = block_levels(stream_key, shape, shards, -0.22, 0.18) if shards else 1.0
    drawn = jax.random.normal(stream_key, shape, jnp.float32) * scale * gain
    return jnp.minimum(jnp.maximum(drawn, -most), most).astype(dtype)


def setup_inputs(seed: int = 0, part: int = 0) -> dict:
    key_list = jax.random.split(jax.random.key(seed), 6)
    part_keys = jax.random.split(jax.random.fold_in(key_list[5], part), 6)
    return {
        "latents": centred(part_keys[0], (FRAMES, H, W, C), 1.0, 6.0, ((0, 4), (1, 4))),
        "weight_in": centred(key_list[1], (3, 3, C, C), (9 * C) ** -0.5, 0.125),
        "weight_out": centred(key_list[2], (3, 3, C, C), (9 * C * 32) ** -0.5, 0.0234375),
        "decay_table": jnp.clip(jax.random.uniform(key_list[3], (LEVELS,), jnp.float32, 0.99, 0.999), 0.99, 0.999),
        "decay_index": place_ends(jax.random.randint(key_list[4], (C,), 0, LEVELS), jax.random.fold_in(key_list[4], 1), 0, LEVELS - 1).astype(jnp.int32),
    }


def convolve(source, weight):
    padded = jnp.pad(source, ((0, 0), (1, 1), (1, 1), (0, 0)))
    height = source.shape[1]
    width = source.shape[2]
    depth = weight.shape[2]

    def one_frame(image):
        total = jnp.zeros((height * width, weight.shape[3]), jnp.float32)
        for tap_row in range(3):
            for tap_col in range(3):
                window = image[tap_row:tap_row + height, tap_col:tap_col + width, :].reshape(-1, depth)
                total = total + jnp.dot(window, weight[tap_row, tap_col], preferred_element_type=jnp.float32)
        return total.reshape(height, width, weight.shape[3])

    return lax.map(one_frame, padded)


def reference(latents, weight_in, weight_out, decay_table, decay_index):
    decays = decay_table[decay_index.astype(jnp.int32)]
    driven = convolve(latents, weight_in)

    def advance(running, incoming):
        running = decays * running + incoming
        return running, running

    start = jnp.zeros(latents.shape[1:], jnp.float32)
    _, states = lax.scan(advance, start, driven)
    rounded = states.astype(jnp.bfloat16)
    mixed = convolve(rounded, weight_out)
    return (latents.astype(jnp.float32) + jax.nn.gelu(mixed)).astype(jnp.bfloat16)
```

```python
import functools

import jax
import jax.numpy as jnp
from jax import lax
from jax.experimental import pallas as pl
from jax.experimental.pallas import tpu as pltpu
from jax.sharding import PartitionSpec as P

MESH = pl.DeviceIdType.MESH
PIECES = 2


def kernel(
    positions,
    strips,
    lat_hbm,
    win_hbm,
    wout_hbm,
    table_ref,
    index_ref,
    out_hbm,
    lat,
    win,
    wout,
    halo,
    wide,
    partial,
    carry,
    passed,
    rounded,
    state_halo,
    wide_states,
    result,
    load_sem,
    store_sem,
    halo_send,
    halo_recv,
    state_send,
    state_recv,
    carry_send,
    carry_recv,
):
    frames, strip, width, channels = lat.shape
    row = lax.axis_index("rows")
    moment = lax.axis_index("tm")
    has_up, has_down = row > 0, row < strips - 1
    has_before, has_after = moment > 0, moment < positions - 1
    span = width // PIECES

    load_lat = pltpu.make_async_copy(lat_hbm, lat, load_sem.at[0])
    load_win = pltpu.make_async_copy(win_hbm, win, load_sem.at[1])
    load_wout = pltpu.make_async_copy(wout_hbm, wout, load_sem.at[2])
    load_lat.start()
    load_win.start()
    load_wout.start()

    barrier = pltpu.get_barrier_semaphore()
    near = (
        (has_up, {"rows": row - 1}),
        (has_down, {"rows": row + 1}),
        (has_before, {"tm": moment - 1}),
        (has_after, {"tm": moment + 1}),
    )
    total = 0
    for exists, where in near:
        total = total + exists.astype(jnp.int32)

        @pl.when(exists)
        def _():
            pl.semaphore_signal(barrier, inc=1, device_id=where, device_id_type=MESH)

    pl.semaphore_wait(barrier, total)

    def halo_copy(side):
        source = lat_hbm.at[:, strip - 1] if side == 0 else lat_hbm.at[:, 0]
        target = row + 1 if side == 0 else row - 1
        return pltpu.make_async_remote_copy(
            src_ref=source,
            dst_ref=halo.at[side],
            send_sem=halo_send.at[side],
            recv_sem=halo_recv.at[side],
            device_id={"rows": target},
            device_id_type=MESH,
        )

    def state_copy(side):
        source = rounded.at[strip - 1] if side == 0 else rounded.at[0]
        target = row + 1 if side == 0 else row - 1
        return pltpu.make_async_remote_copy(
            src_ref=source,
            dst_ref=state_halo.at[side],
            send_sem=state_send.at[side],
            recv_sem=state_recv.at[side],
            device_id={"rows": target},
            device_id_type=MESH,
        )

    def carry_copy(i, piece):
        part = pl.ds(piece * span, span)
        return pltpu.make_async_remote_copy(
            src_ref=passed.at[i, part],
            dst_ref=carry.at[i, part],
            send_sem=carry_send.at[i, piece],
            recv_sem=carry_recv.at[i, piece],
            device_id={"tm": moment + 1},
            device_id_type=MESH,
        )

    @pl.when(has_down)
    def _():
        halo_copy(0).start()

    @pl.when(has_up)
    def _():
        halo_copy(1).start()

    chosen = index_ref[...]
    decays = jnp.zeros(chosen.shape, jnp.float32)
    for level in range(table_ref.shape[0]):
        decays = jnp.where(chosen == level, table_ref[level], decays)
    growth = [decays]
    for _ in range(frames - 1):
        growth.append(growth[-1] * decays)

    column = lax.broadcasted_iota(jnp.int32, (width, channels), 0)

    def spread(target, place, frame, value):
        full = value.astype(jnp.float32)
        before = jnp.where(column == 0, 0.0, pltpu.roll(full, 1, 0))
        after = jnp.where(column == width - 1, 0.0, pltpu.roll(full, width - 1, 0))
        target[place, frame, :, 0:channels] = before.astype(jnp.bfloat16)
        target[place, frame, :, channels : 2 * channels] = value
        target[place, frame, :, 2 * channels : 3 * channels] = after.astype(jnp.bfloat16)

    def border(target, place, buffer, side, exists, arrival):
        @pl.when(exists)
        def _():
            arrival.wait_recv()
            for frame in range(frames):
                spread(target, place, frame, buffer[side, frame])

        @pl.when(jnp.logical_not(exists))
        def _():
            target[place] = jnp.zeros(target.shape[1:], target.dtype)

    def convolve(source, weight, i):
        window = jnp.concatenate([source[i], source[i + 1], source[i + 2]], axis=-1)
        flat = window.reshape(frames * width, 9 * channels)
        return jnp.dot(flat, weight[...], preferred_element_type=jnp.float32).reshape(
            frames, width, channels
        )

    def drive(i):
        driven = convolve(wide, win, i)
        running = driven[0]
        partial[i, 0] = running
        for frame in range(1, frames):
            running = decays * running + driven[frame]
            partial[i, frame] = running

    def publish(i):
        for side, edge in ((0, strip - 1), (1, 0)):
            if i == edge:

                @pl.when(has_down if side == 0 else has_up)
                def _():
                    state_copy(side).start()

        for frame in range(frames):
            spread(wide_states, i + 1, frame, rounded[i, frame])

    def first(i):
        @pl.when(jnp.logical_not(has_before))
        def _():
            passed[i] = partial[i, frames - 1].astype(passed.dtype)

            @pl.when(has_after)
            def _():
                for piece in range(PIECES):
                    carry_copy(i, piece).start()

            for frame in range(frames):
                rounded[i, frame] = partial[i, frame].astype(jnp.bfloat16)
            publish(i)

    def later(i):
        @pl.when(has_before)
        def _():
            for piece in range(PIECES):
                part = pl.ds(piece * span, span)
                carry_copy(i, piece).wait_recv()
                arrived = carry[i, part].astype(jnp.float32)
                last = partial[i, frames - 1, part] + growth[frames - 1] * arrived
                passed[i, part] = last.astype(passed.dtype)

                @pl.when(has_after)
                def _():
                    carry_copy(i, piece).start()

                rounded[i, frames - 1, part] = last.astype(jnp.bfloat16)
                for frame in range(frames - 1):
                    state = partial[i, frame, part] + growth[frame] * arrived
                    rounded[i, frame, part] = state.astype(jnp.bfloat16)
            publish(i)

    def emit(i):
        mixed = convolve(wide_states, wout, i)
        for frame in range(frames):
            updated = lat[frame, i].astype(jnp.float32) + jax.nn.gelu(mixed[frame])
            result[frame, i] = updated.astype(jnp.bfloat16)
        pltpu.make_async_copy(result.at[:, i], out_hbm.at[:, i], store_sem.at[i]).start()

    middle = list(range(1, strip - 1))
    edges = [0, strip - 1]

    load_lat.wait()
    for i in range(strip):
        for frame in range(frames):
            spread(wide, i + 1, frame, lat[frame, i])
    load_win.wait()
    for i in middle:
        drive(i)
        first(i)
    border(wide, 0, halo, 0, has_up, halo_copy(0))
    drive(0)
    first(0)
    border(wide, strip + 1, halo, 1, has_down, halo_copy(1))
    drive(strip - 1)
    first(strip - 1)
    load_wout.wait()
    for i in middle + edges:
        later(i)
    for i in middle:
        emit(i)
    border(wide_states, 0, state_halo, 0, has_up, state_copy(0))
    emit(0)
    border(wide_states, strip + 1, state_halo, 1, has_down, state_copy(1))
    emit(strip - 1)

    @pl.when(has_down)
    def _():
        halo_copy(0).wait_send()
        state_copy(0).wait_send()

    @pl.when(has_up)
    def _():
        halo_copy(1).wait_send()
        state_copy(1).wait_send()

    @pl.when(has_after)
    def _():
        for i in range(strip):
            for piece in range(PIECES):
                carry_copy(i, piece).wait_send()

    for i in range(strip):
        pltpu.make_async_copy(result.at[:, i], out_hbm.at[:, i], store_sem.at[i]).wait()


def local(positions, strips, latents, weight_in, weight_out, decay_table, decay_index):
    frames, strip, width, channels = latents.shape
    link = jnp.bfloat16 if positions <= 8 else jnp.float32
    half = jnp.bfloat16
    dma = pltpu.SemaphoreType.DMA
    anywhere = pl.BlockSpec(memory_space=pl.ANY)
    return pl.pallas_call(
        functools.partial(kernel, positions, strips),
        out_shape=jax.ShapeDtypeStruct(latents.shape, latents.dtype),
        in_specs=[
            anywhere,
            anywhere,
            anywhere,
            pl.BlockSpec(memory_space=pltpu.SMEM),
            pl.BlockSpec(memory_space=pltpu.VMEM),
        ],
        out_specs=anywhere,
        scratch_shapes=[
            pltpu.VMEM((frames, strip, width, channels), half),
            pltpu.VMEM((9 * channels, channels), half),
            pltpu.VMEM((9 * channels, channels), half),
            pltpu.VMEM((2, frames, width, channels), half),
            pltpu.VMEM((strip + 2, frames, width, 3 * channels), half),
            pltpu.VMEM((strip, frames, width, channels), jnp.float32),
            pltpu.VMEM((strip, width, channels), link),
            pltpu.VMEM((strip, width, channels), link),
            pltpu.VMEM((strip, frames, width, channels), half),
            pltpu.VMEM((2, frames, width, channels), half),
            pltpu.VMEM((strip + 2, frames, width, 3 * channels), half),
            pltpu.VMEM((frames, strip, width, channels), half),
            dma((3,)),
            dma((strip,)),
            dma((2,)),
            dma((2,)),
            dma((2,)),
            dma((2,)),
            dma((strip, PIECES)),
            dma((strip, PIECES)),
        ],
        compiler_params=pltpu.CompilerParams(collective_id=0, has_side_effects=True),
    )(
        latents,
        weight_in.reshape(9 * channels, channels),
        weight_out.reshape(9 * channels, channels),
        decay_table,
        decay_index.reshape(1, channels),
    )


def solution(mesh):
    in_specs = (P(("groups", "tm"), "rows", None, None), P(), P(), P(), P())
    out_specs = P(("groups", "tm"), "rows", None, None)
    body = functools.partial(local, mesh.shape["tm"], mesh.shape["rows"])
    return jax.shard_map(body, mesh=mesh, in_specs=in_specs, out_specs=out_specs, check_vma=False)
```

```python
import functools

import jax
import jax.numpy as jnp
from jax import lax
from jax.experimental import pallas as pl
from jax.experimental.pallas import tpu as pltpu
from jax.sharding import PartitionSpec as P

MESH = pl.DeviceIdType.MESH
PIECES = 2


def kernel(
    positions,
    strips,
    lat_hbm,
    win_hbm,
    wout_hbm,
    table_ref,
    index_ref,
    out_hbm,
    lat,
    win,
    wout,
    halo,
    wide,
    partial,
    carry,
    passed,
    rounded,
    state_halo,
    wide_states,
    result,
    load_sem,
    store_sem,
    halo_send,
    halo_recv,
    state_send,
    state_recv,
    carry_send,
    carry_recv,
):
    frames, strip, width, channels = lat.shape
    row = lax.axis_index("rows")
    moment = lax.axis_index("tm")
    has_up, has_down = row > 0, row < strips - 1
    has_before, has_after = moment > 0, moment < positions - 1
    span = width // PIECES

    load_lat = pltpu.make_async_copy(lat_hbm, lat, load_sem.at[0])
    load_win = pltpu.make_async_copy(win_hbm, win, load_sem.at[1])
    load_wout = pltpu.make_async_copy(wout_hbm, wout, load_sem.at[2])
    load_lat.start()
    load_win.start()
    load_wout.start()

    barrier = pltpu.get_barrier_semaphore()
    near = (
        (has_up, {"rows": row - 1}),
        (has_down, {"rows": row + 1}),
        (has_before, {"tm": moment - 1}),
        (has_after, {"tm": moment + 1}),
    )
    total = 0
    for exists, where in near:
        total = total + exists.astype(jnp.int32)

        @pl.when(exists)
        def _():
            pl.semaphore_signal(barrier, inc=1, device_id=where, device_id_type=MESH)

    pl.semaphore_wait(barrier, total)

    def halo_copy(side):
        source = lat_hbm.at[:, strip - 1] if side == 0 else lat_hbm.at[:, 0]
        target = row + 1 if side == 0 else row - 1
        return pltpu.make_async_remote_copy(
            src_ref=source,
            dst_ref=halo.at[side],
            send_sem=halo_send.at[side],
            recv_sem=halo_recv.at[side],
            device_id={"rows": target},
            device_id_type=MESH,
        )

    def state_copy(side):
        source = rounded.at[strip - 1] if side == 0 else rounded.at[0]
        target = row + 1 if side == 0 else row - 1
        return pltpu.make_async_remote_copy(
            src_ref=source,
            dst_ref=state_halo.at[side],
            send_sem=state_send.at[side],
            recv_sem=state_recv.at[side],
            device_id={"rows": target},
            device_id_type=MESH,
        )

    def carry_copy(i, piece):
        part = pl.ds(piece * span, span)
        return pltpu.make_async_remote_copy(
            src_ref=passed.at[i, part],
            dst_ref=carry.at[i, part],
            send_sem=carry_send.at[i, piece],
            recv_sem=carry_recv.at[i, piece],
            device_id={"tm": moment + 1},
            device_id_type=MESH,
        )

    @pl.when(has_down)
    def _():
        halo_copy(0).start()

    @pl.when(has_up)
    def _():
        halo_copy(1).start()

    chosen = index_ref[...]
    decays = jnp.zeros(chosen.shape, jnp.float32)
    for level in range(table_ref.shape[0]):
        decays = jnp.where(chosen == level, table_ref[level], decays)
    growth = [decays]
    for _ in range(frames - 1):
        growth.append(growth[-1] * decays)

    column = lax.broadcasted_iota(jnp.int32, (width, channels), 0)

    def spread(target, place, frame, value):
        full = value.astype(jnp.float32)
        before = jnp.where(column == 0, 0.0, pltpu.roll(full, 1, 0))
        after = jnp.where(column == width - 1, 0.0, pltpu.roll(full, width - 1, 0))
        target[place, frame, :, 0:channels] = before.astype(jnp.bfloat16)
        target[place, frame, :, channels : 2 * channels] = value
        target[place, frame, :, 2 * channels : 3 * channels] = after.astype(jnp.bfloat16)

    def border(target, place, buffer, side, exists, arrival):
        @pl.when(exists)
        def _():
            arrival.wait_recv()
            for frame in range(frames):
                spread(target, place, frame, buffer[side, frame])

        @pl.when(jnp.logical_not(exists))
        def _():
            target[place] = jnp.zeros(target.shape[1:], target.dtype)

    def convolve(source, weight, i):
        window = jnp.concatenate([source[i], source[i + 1], source[i + 2]], axis=-1)
        flat = window.reshape(frames * width, 9 * channels)
        return jnp.dot(flat, weight[...], preferred_element_type=jnp.float32).reshape(
            frames, width, channels
        )

    def drive(i):
        driven = convolve(wide, win, i)
        running = driven[0]
        partial[i, 0] = running
        for frame in range(1, frames):
            running = decays * running + driven[frame]
            partial[i, frame] = running

    def publish(i):
        for side, edge in ((0, strip - 1), (1, 0)):
            if i == edge:

                @pl.when(has_down if side == 0 else has_up)
                def _():
                    state_copy(side).start()

        for frame in range(frames):
            spread(wide_states, i + 1, frame, rounded[i, frame])

    def first(i):
        @pl.when(jnp.logical_not(has_before))
        def _():
            passed[i] = partial[i, frames - 1].astype(passed.dtype)

            @pl.when(has_after)
            def _():
                for piece in range(PIECES):
                    carry_copy(i, piece).start()

            for frame in range(frames):
                rounded[i, frame] = partial[i, frame].astype(jnp.bfloat16)
            publish(i)

    def later(i):
        @pl.when(has_before)
        def _():
            for piece in range(PIECES):
                part = pl.ds(piece * span, span)
                carry_copy(i, piece).wait_recv()
                arrived = carry[i, part].astype(jnp.float32)
                last = partial[i, frames - 1, part] + growth[frames - 1] * arrived
                passed[i, part] = last.astype(passed.dtype)

                @pl.when(has_after)
                def _():
                    carry_copy(i, piece).start()

                rounded[i, frames - 1, part] = last.astype(jnp.bfloat16)
                for frame in range(frames - 1):
                    state = partial[i, frame, part] + growth[frame] * arrived
                    rounded[i, frame, part] = state.astype(jnp.bfloat16)
            publish(i)

    def emit(i):
        mixed = convolve(wide_states, wout, i)
        for frame in range(frames):
            updated = lat[frame, i].astype(jnp.float32) + jax.nn.gelu(mixed[frame])
            result[frame, i] = updated.astype(jnp.bfloat16)
        pltpu.make_async_copy(result.at[:, i], out_hbm.at[:, i], store_sem.at[i]).start()

    middle = list(range(1, strip - 1))
    edges = [0, strip - 1]

    load_lat.wait()
    for i in range(strip):
        for frame in range(frames):
            spread(wide, i + 1, frame, lat[frame, i])
    load_win.wait()
    for i in middle:
        drive(i)
        first(i)
    border(wide, 0, halo, 0, has_up, halo_copy(0))
    drive(0)
    first(0)
    border(wide, strip + 1, halo, 1, has_down, halo_copy(1))
    drive(strip - 1)
    first(strip - 1)
    load_wout.wait()
    for i in middle + edges:
        later(i)
    for i in middle:
        emit(i)
    border(wide_states, 0, state_halo, 0, has_up, state_copy(0))
    emit(0)
    border(wide_states, strip + 1, state_halo, 1, has_down, state_copy(1))
    emit(strip - 1)

    @pl.when(has_down)
    def _():
        halo_copy(0).wait_send()
        state_copy(0).wait_send()

    @pl.when(has_up)
    def _():
        halo_copy(1).wait_send()
        state_copy(1).wait_send()

    @pl.when(has_after)
    def _():
        for i in range(strip):
            for piece in range(PIECES):
                carry_copy(i, piece).wait_send()

    for i in range(strip):
        pltpu.make_async_copy(result.at[:, i], out_hbm.at[:, i], store_sem.at[i]).wait()


def local(positions, strips, latents, weight_in, weight_out, decay_table, decay_index):
    frames, strip, width, channels = latents.shape
    link = jnp.bfloat16 if positions <= 8 else jnp.float32
    half = jnp.bfloat16
    dma = pltpu.SemaphoreType.DMA
    anywhere = pl.BlockSpec(memory_space=pl.ANY)
    return pl.pallas_call(
        functools.partial(kernel, positions, strips),
        out_shape=jax.ShapeDtypeStruct(latents.shape, latents.dtype),
        in_specs=[
            pl.BlockSpec(memory_space=pltpu.HBM),
            pl.BlockSpec(memory_space=pltpu.HBM),
            pl.BlockSpec(memory_space=pltpu.HBM),
            pl.BlockSpec(memory_space=pltpu.SMEM),
            pl.BlockSpec(memory_space=pltpu.VMEM),
        ],
        out_specs=anywhere,
        scratch_shapes=[
            pltpu.VMEM((frames, strip, width, channels), half),
            pltpu.VMEM((9 * channels, channels), half),
            pltpu.VMEM((9 * channels, channels), half),
            pltpu.VMEM((2, frames, width, channels), half),
            pltpu.VMEM((strip + 2, frames, width, 3 * channels), half),
            pltpu.VMEM((strip, frames, width, channels), jnp.float32),
            pltpu.VMEM((strip, width, channels), link),
            pltpu.VMEM((strip, width, channels), link),
            pltpu.VMEM((strip, frames, width, channels), half),
            pltpu.VMEM((2, frames, width, channels), half),
            pltpu.VMEM((strip + 2, frames, width, 3 * channels), half),
            pltpu.VMEM((frames, strip, width, channels), half),
            dma((3,)),
            dma((strip,)),
            dma((2,)),
            dma((2,)),
            dma((2,)),
            dma((2,)),
            dma((strip, PIECES)),
            dma((strip, PIECES)),
        ],
        compiler_params=pltpu.CompilerParams(collective_id=0, has_side_effects=True, vmem_limit_bytes=32 * 1024 * 1024),
    )(
        latents,
        weight_in.reshape(9 * channels, channels),
        weight_out.reshape(9 * channels, channels),
        decay_table,
        decay_index.reshape(1, channels),
    )


def solution(mesh):
    in_specs = (P(("groups", "tm"), "rows", None, None), P(), P(), P(), P())
    out_specs = P(("groups", "tm"), "rows", None, None)
    body = functools.partial(local, mesh.shape["tm"], mesh.shape["rows"])
    return jax.shard_map(body, mesh=mesh, in_specs=in_specs, out_specs=out_specs, check_vma=False)
```

```python
import functools

import jax
import jax.numpy as jnp
from jax import lax
from jax.experimental import pallas as pl
from jax.experimental.pallas import tpu as pltpu
from jax.sharding import PartitionSpec as P

MESH = pl.DeviceIdType.MESH
PIECES = 2


def kernel(
    positions,
    strips,
    lat_hbm,
    win_hbm,
    wout_hbm,
    table_ref,
    index_ref,
    out_hbm,
    lat,
    win,
    wout,
    halo,
    wide,
    partial,
    carry,
    passed,
    rounded,
    state_halo,
    relayed,
    mixed,
    wide_states,
    result,
    load_sem,
    store_sem,
    halo_send,
    halo_recv,
    state_send,
    state_recv,
    carry_send,
    carry_recv,
    relay_send,
    relay_recv,
):
    frames, strip, width, channels = lat.shape
    row = lax.axis_index("rows")
    moment = lax.axis_index("tm")
    has_up, has_down = row > 0, row < strips - 1
    has_before, has_after = moment > 0, moment < positions - 1
    span = width // PIECES

    load_lat = pltpu.make_async_copy(lat_hbm, lat, load_sem.at[0])
    load_win = pltpu.make_async_copy(win_hbm, win, load_sem.at[1])
    load_wout = pltpu.make_async_copy(wout_hbm, wout, load_sem.at[2])

    barrier = pltpu.get_barrier_semaphore()
    near = (
        (has_up, {"rows": row - 1}),
        (has_down, {"rows": row + 1}),
        (has_before, {"tm": moment - 1}),
        (has_after, {"tm": moment + 1}),
    )
    total = 0
    for exists, where in near:
        total = total + exists.astype(jnp.int32)

        @pl.when(exists)
        def _():
            pl.semaphore_signal(barrier, inc=1, device_id=where, device_id_type=MESH)

    load_lat.start()
    load_win.start()
    load_wout.start()
    pl.semaphore_wait(barrier, total)

    def halo_copy(side):
        source = lat_hbm.at[:, strip - 1] if side == 0 else lat_hbm.at[:, 0]
        target = row + 1 if side == 0 else row - 1
        return pltpu.make_async_remote_copy(
            src_ref=source,
            dst_ref=halo.at[side],
            send_sem=halo_send.at[side],
            recv_sem=halo_recv.at[side],
            device_id={"rows": target},
            device_id_type=MESH,
        )

    def state_copy(side):
        source = rounded.at[strip - 1] if side == 0 else rounded.at[0]
        target = row + 1 if side == 0 else row - 1
        return pltpu.make_async_remote_copy(
            src_ref=source,
            dst_ref=state_halo.at[side],
            send_sem=state_send.at[side],
            recv_sem=state_recv.at[side],
            device_id={"rows": target},
            device_id_type=MESH,
        )

    def relay_copy(side, piece):
        part = pl.ds(piece * span, span)
        edge = strip - 1 if side == 0 else 0
        target = row + 1 if side == 0 else row - 1
        return pltpu.make_async_remote_copy(
            src_ref=carry.at[edge, part],
            dst_ref=relayed.at[side, part],
            send_sem=relay_send.at[side, piece],
            recv_sem=relay_recv.at[side, piece],
            device_id={"rows": target},
            device_id_type=MESH,
        )

    def carry_copy(i, piece):
        part = pl.ds(piece * span, span)
        return pltpu.make_async_remote_copy(
            src_ref=passed.at[i, part],
            dst_ref=carry.at[i, part],
            send_sem=carry_send.at[i, piece],
            recv_sem=carry_recv.at[i, piece],
            device_id={"tm": moment + 1},
            device_id_type=MESH,
        )

    @pl.when(has_down)
    def _():
        halo_copy(0).start()

    @pl.when(has_up)
    def _():
        halo_copy(1).start()

    chosen = index_ref[...]
    decays = jnp.zeros(chosen.shape, jnp.float32)
    for level in range(table_ref.shape[0]):
        decays = jnp.where(chosen == level, table_ref[level], decays)
    growth = [decays]
    for _ in range(frames - 1):
        growth.append(growth[-1] * decays)

    column = lax.broadcasted_iota(jnp.int32, (width, channels), 0)

    def spread(target, place, frame, value):
        full = value.astype(jnp.float32)
        before = jnp.where(column == 0, 0.0, pltpu.roll(full, 1, 0))
        after = jnp.where(column == width - 1, 0.0, pltpu.roll(full, width - 1, 0))
        target[place, frame, :, 0:channels] = before.astype(jnp.bfloat16)
        target[place, frame, :, channels : 2 * channels] = value
        target[place, frame, :, 2 * channels : 3 * channels] = after.astype(jnp.bfloat16)

    def border(i, side, exists):
        @pl.when(exists)
        def _():
            halo_copy(side).wait_recv()
            for frame in range(frames):
                spread(wide, i, frame, halo[side, frame])

        @pl.when(jnp.logical_not(exists))
        def _():
            wide[i] = jnp.zeros(wide.shape[1:], wide.dtype)

    def drive(i):
        window = jnp.concatenate([wide[i], wide[i + 1], wide[i + 2]], axis=-1)
        flat = window.reshape(frames * width, 9 * channels)
        driven = jnp.dot(flat, win[...], preferred_element_type=jnp.float32).reshape(
            frames, width, channels
        )
        running = driven[0]
        partial[i, 0] = running
        for frame in range(1, frames):
            running = decays * running + driven[frame]
            partial[i, frame] = running

        @pl.when(jnp.logical_not(has_before))
        def _():
            passed[i] = partial[i, frames - 1].astype(passed.dtype)

            @pl.when(has_after)
            def _():
                for piece in range(PIECES):
                    carry_copy(i, piece).start()

    def settle(i, side, exists):
        for frame in range(frames):
            rounded[i, frame] = partial[i, frame].astype(jnp.bfloat16)

        @pl.when(exists)
        def _():
            state_copy(side).start()

    def advance(i, side=None, exists=None):
        for piece in range(PIECES):
            part = pl.ds(piece * span, span)
            carry_copy(i, piece).wait_recv()
            if side is not None:

                @pl.when(exists)
                def _():
                    relay_copy(side, piece).start()

            arrived = carry[i, part].astype(jnp.float32)
            last = partial[i, frames - 1, part] + growth[frames - 1] * arrived
            passed[i, part] = last.astype(passed.dtype)

            @pl.when(has_after)
            def _():
                carry_copy(i, piece).start()

            partial[i, frames - 1, part] = last
            for frame in range(frames - 1):
                partial[i, frame, part] = partial[i, frame, part] + growth[frame] * arrived

    def stretch(i):
        for frame in range(frames):
            spread(wide_states, i + 1, frame, partial[i, frame].astype(jnp.bfloat16))

    def outer(place, side, exists):
        @pl.when(exists)
        def _():
            state_copy(side).wait_recv()

            @pl.when(has_before)
            def _():
                for piece in range(PIECES):
                    relay_copy(side, piece).wait_recv()
                arrived = relayed[side].astype(jnp.float32)
                for frame in range(frames):
                    state = state_halo[side, frame].astype(jnp.float32)
                    state = state + growth[frame] * arrived
                    spread(wide_states, place, frame, state.astype(jnp.bfloat16))

            @pl.when(jnp.logical_not(has_before))
            def _():
                for frame in range(frames):
                    spread(wide_states, place, frame, state_halo[side, frame])

    def product(i, low, high):
        window = [wide_states[i + tap] for tap in range(low, high)]
        window = window[0] if high == low + 1 else jnp.concatenate(window, axis=-1)
        flat = window.reshape(frames * width, (high - low) * 3 * channels)
        taps = wout[low * 3 * channels : high * 3 * channels]
        value = jnp.dot(flat, taps, preferred_element_type=jnp.float32)
        return value.reshape(frames, width, channels)

    def write(i, value):
        for frame in range(frames):
            updated = lat[frame, i].astype(jnp.float32) + jax.nn.gelu(value[frame])
            result[frame, i] = updated.astype(jnp.bfloat16)
        pltpu.make_async_copy(result.at[:, i], out_hbm.at[:, i], store_sem.at[i]).start()

    def close(side, exists):
        i, place, low = (0, 0, 0) if side == 0 else (strip - 1, strip + 1, 2)
        outer(place, side, exists)

        @pl.when(exists)
        def _():
            write(i, mixed[side] + product(i, low, low + 1))

        @pl.when(jnp.logical_not(exists))
        def _():
            write(i, mixed[side])

    middle = list(range(1, strip - 1))
    bottom = strip - 1

    load_lat.wait()
    for i in range(strip):
        for frame in range(frames):
            spread(wide, i + 1, frame, lat[frame, i])
    load_win.wait()
    even = lax.rem(row, 2) == 0

    def drive_top():
        border(0, 0, has_up)
        drive(0)
        settle(0, 1, has_up)

    def drive_bottom():
        border(strip + 1, 1, has_down)
        drive(bottom)
        settle(bottom, 0, has_down)

    def by_parity(one, two):
        @pl.when(even)
        def _():
            one()

        @pl.when(jnp.logical_not(even))
        def _():
            two()

    for i in middle[:1]:
        drive(i)
    by_parity(drive_bottom, drive_top)
    by_parity(drive_top, drive_bottom)
    for i in middle[1:]:
        drive(i)

    @pl.when(has_before)
    def _():
        for i in middle[:1]:
            advance(i)
        for i in middle[:1]:
            stretch(i)

        def low_first():
            advance(bottom, 0, has_down)
            advance(0, 1, has_up)

        def high_first():
            advance(0, 1, has_up)
            advance(bottom, 0, has_down)

        by_parity(low_first, high_first)

    load_wout.wait()

    @pl.when(jnp.logical_not(has_before))
    def _():
        for i in middle[:1]:
            stretch(i)

    stretch(0)
    stretch(bottom)
    mixed[0] = product(0, 1, 3)

    @pl.when(has_before)
    def _():
        for i in middle[1:]:
            advance(i)

    for i in middle[1:]:
        stretch(i)
    mixed[1] = product(bottom, 0, 2)
    for i in middle:
        write(i, product(i, 0, 3))

    def top_last():
        close(1, has_down)
        close(0, has_up)

    def bottom_last():
        close(0, has_up)
        close(1, has_down)

    by_parity(top_last, bottom_last)

    @pl.when(has_down)
    def _():
        halo_copy(0).wait_send()
        state_copy(0).wait_send()

    @pl.when(has_up)
    def _():
        halo_copy(1).wait_send()
        state_copy(1).wait_send()

    @pl.when(jnp.logical_and(has_down, has_before))
    def _():
        for piece in range(PIECES):
            relay_copy(0, piece).wait_send()

    @pl.when(jnp.logical_and(has_up, has_before))
    def _():
        for piece in range(PIECES):
            relay_copy(1, piece).wait_send()

    @pl.when(has_after)
    def _():
        for i in range(strip):
            for piece in range(PIECES):
                carry_copy(i, piece).wait_send()

    for i in range(strip):
        pltpu.make_async_copy(result.at[:, i], out_hbm.at[:, i], store_sem.at[i]).wait()


def local(positions, strips, latents, weight_in, weight_out, decay_table, decay_index):
    frames, strip, width, channels = latents.shape
    link = jnp.bfloat16 if positions <= 8 else jnp.float32
    half = jnp.bfloat16
    dma = pltpu.SemaphoreType.DMA
    anywhere = pl.BlockSpec(memory_space=pl.ANY)
    return pl.pallas_call(
        functools.partial(kernel, positions, strips),
        out_shape=jax.ShapeDtypeStruct(latents.shape, latents.dtype),
        in_specs=[
            anywhere,
            anywhere,
            anywhere,
            pl.BlockSpec(memory_space=pltpu.SMEM),
            pl.BlockSpec(memory_space=pltpu.VMEM),
        ],
        out_specs=anywhere,
        scratch_shapes=[
            pltpu.VMEM((frames, strip, width, channels), half),
            pltpu.VMEM((9 * channels, channels), half),
            pltpu.VMEM((9 * channels, channels), half),
            pltpu.VMEM((2, frames, width, channels), half),
            pltpu.VMEM((strip + 2, frames, width, 3 * channels), half),
            pltpu.VMEM((strip, frames, width, channels), jnp.float32),
            pltpu.VMEM((strip, width, channels), link),
            pltpu.VMEM((strip, width, channels), link),
            pltpu.VMEM((strip, frames, width, channels), half),
            pltpu.VMEM((2, frames, width, channels), half),
            pltpu.VMEM((2, width, channels), link),
            pltpu.VMEM((2, frames, width, channels), jnp.float32),
            pltpu.VMEM((strip + 2, frames, width, 3 * channels), half),
            pltpu.VMEM((frames, strip, width, channels), half),
            dma((3,)),
            dma((strip,)),
            dma((2,)),
            dma((2,)),
            dma((2,)),
            dma((2,)),
            dma((strip, PIECES)),
            dma((strip, PIECES)),
            dma((2, PIECES)),
            dma((2, PIECES)),
        ],
        compiler_params=pltpu.CompilerParams(collective_id=0, has_side_effects=True),
    )(
        latents,
        weight_in.reshape(9 * channels, channels),
        weight_out.reshape(9 * channels, channels),
        decay_table,
        decay_index.reshape(1, channels),
    )


def solution(mesh):
    in_specs = (P(("groups", "tm"), "rows", None, None), P(), P(), P(), P())
    out_specs = P(("groups", "tm"), "rows", None, None)
    body = functools.partial(local, mesh.shape["tm"], mesh.shape["rows"])
    return jax.shard_map(body, mesh=mesh, in_specs=in_specs, out_specs=out_specs, check_vma=False)
```

```python
import functools

import jax
import jax.numpy as jnp
from jax import lax
from jax.experimental import pallas as pl
from jax.experimental.pallas import tpu as pltpu
from jax.sharding import PartitionSpec as P

MESH = pl.DeviceIdType.MESH
PIECES = 4


def kernel(
    positions,
    strips,
    lat_hbm,
    win_hbm,
    wout_hbm,
    table_ref,
    index_ref,
    out_hbm,
    lat,
    win,
    wout,
    halo,
    wide,
    partial,
    carry,
    passed,
    rounded,
    state_halo,
    relayed,
    mixed,
    wide_states,
    result,
    load_sem,
    store_sem,
    halo_send,
    halo_recv,
    state_send,
    state_recv,
    carry_send,
    carry_recv,
    relay_send,
    relay_recv,
):
    frames, strip, width, channels = lat.shape
    row = lax.axis_index("rows")
    moment = lax.axis_index("tm")
    has_up, has_down = row > 0, row < strips - 1
    has_before, has_after = moment > 0, moment < positions - 1
    span = width // PIECES

    load_lat = pltpu.make_async_copy(lat_hbm, lat, load_sem.at[0])
    load_win = pltpu.make_async_copy(win_hbm, win, load_sem.at[1])
    load_wout = pltpu.make_async_copy(wout_hbm, wout, load_sem.at[2])

    barrier = pltpu.get_barrier_semaphore()
    near = (
        (has_up, {"rows": row - 1}),
        (has_down, {"rows": row + 1}),
        (has_before, {"tm": moment - 1}),
        (has_after, {"tm": moment + 1}),
    )
    total = 0
    for exists, where in near:
        total = total + exists.astype(jnp.int32)

        @pl.when(exists)
        def _():
            pl.semaphore_signal(barrier, inc=1, device_id=where, device_id_type=MESH)

    load_lat.start()
    load_win.start()
    load_wout.start()
    pl.semaphore_wait(barrier, total)

    def halo_copy(side):
        source = lat_hbm.at[:, strip - 1] if side == 0 else lat_hbm.at[:, 0]
        target = row + 1 if side == 0 else row - 1
        return pltpu.make_async_remote_copy(
            src_ref=source,
            dst_ref=halo.at[side],
            send_sem=halo_send.at[side],
            recv_sem=halo_recv.at[side],
            device_id={"rows": target},
            device_id_type=MESH,
        )

    def state_copy(side):
        source = rounded.at[strip - 1] if side == 0 else rounded.at[0]
        target = row + 1 if side == 0 else row - 1
        return pltpu.make_async_remote_copy(
            src_ref=source,
            dst_ref=state_halo.at[side],
            send_sem=state_send.at[side],
            recv_sem=state_recv.at[side],
            device_id={"rows": target},
            device_id_type=MESH,
        )

    def relay_copy(side, piece):
        part = pl.ds(piece * span, span)
        edge = strip - 1 if side == 0 else 0
        target = row + 1 if side == 0 else row - 1
        return pltpu.make_async_remote_copy(
            src_ref=carry.at[edge, part],
            dst_ref=relayed.at[side, part],
            send_sem=relay_send.at[side, piece],
            recv_sem=relay_recv.at[side, piece],
            device_id={"rows": target},
            device_id_type=MESH,
        )

    def carry_copy(i, piece):
        part = pl.ds(piece * span, span)
        return pltpu.make_async_remote_copy(
            src_ref=passed.at[i, part],
            dst_ref=carry.at[i, part],
            send_sem=carry_send.at[i, piece],
            recv_sem=carry_recv.at[i, piece],
            device_id={"tm": moment + 1},
            device_id_type=MESH,
        )

    even = lax.rem(row, 2) == 0

    @pl.when(jnp.logical_and(has_up, even))
    def _():
        halo_copy(1).start()

    @pl.when(has_down)
    def _():
        halo_copy(0).start()

    @pl.when(jnp.logical_and(has_up, jnp.logical_not(even)))
    def _():
        halo_copy(1).start()

    chosen = index_ref[...]
    decays = jnp.zeros(chosen.shape, jnp.float32)
    for level in range(table_ref.shape[0]):
        decays = jnp.where(chosen == level, table_ref[level], decays)
    growth = [decays]
    for _ in range(frames - 1):
        growth.append(growth[-1] * decays)

    column = lax.broadcasted_iota(jnp.int32, (width, channels), 0)

    def spread(target, place, frame, value):
        full = value.astype(jnp.float32)
        before = jnp.where(column == 0, 0.0, pltpu.roll(full, 1, 0))
        after = jnp.where(column == width - 1, 0.0, pltpu.roll(full, width - 1, 0))
        target[place, frame, :, 0:channels] = before.astype(jnp.bfloat16)
        target[place, frame, :, channels : 2 * channels] = value
        target[place, frame, :, 2 * channels : 3 * channels] = after.astype(jnp.bfloat16)

    def border(i, side, exists):
        @pl.when(exists)
        def _():
            halo_copy(side).wait_recv()
            for frame in range(frames):
                spread(wide, i, frame, halo[side, frame])

        @pl.when(jnp.logical_not(exists))
        def _():
            wide[i] = jnp.zeros(wide.shape[1:], wide.dtype)

    def drive(i):
        window = jnp.concatenate([wide[i], wide[i + 1], wide[i + 2]], axis=-1)
        flat = window.reshape(frames * width, 9 * channels)
        driven = jnp.dot(flat, win[...], preferred_element_type=jnp.float32).reshape(
            frames, width, channels
        )
        running = driven[0]
        partial[i, 0] = running
        for frame in range(1, frames):
            running = decays * running + driven[frame]
            partial[i, frame] = running

        @pl.when(jnp.logical_not(has_before))
        def _():
            passed[i] = partial[i, frames - 1].astype(passed.dtype)

            @pl.when(has_after)
            def _():
                for piece in range(PIECES):
                    carry_copy(i, piece).start()

    def settle(i, side, exists):
        for frame in range(frames):
            rounded[i, frame] = partial[i, frame].astype(jnp.bfloat16)

        @pl.when(exists)
        def _():
            state_copy(side).start()

    def advance(i, side=None, exists=None):
        for piece in range(PIECES):
            part = pl.ds(piece * span, span)
            carry_copy(i, piece).wait_recv()
            if side is not None:

                @pl.when(exists)
                def _():
                    relay_copy(side, piece).start()

            arrived = carry[i, part].astype(jnp.float32)
            last = partial[i, frames - 1, part] + growth[frames - 1] * arrived
            passed[i, part] = last.astype(passed.dtype)

            @pl.when(has_after)
            def _():
                carry_copy(i, piece).start()

            partial[i, frames - 1, part] = last
            for frame in range(frames - 1):
                partial[i, frame, part] = partial[i, frame, part] + growth[frame] * arrived

    def stretch(i):
        for frame in range(frames):
            spread(wide_states, i + 1, frame, partial[i, frame].astype(jnp.bfloat16))

    def outer(place, side, exists):
        @pl.when(exists)
        def _():
            state_copy(side).wait_recv()

            @pl.when(has_before)
            def _():
                for piece in range(PIECES):
                    relay_copy(side, piece).wait_recv()
                arrived = relayed[side].astype(jnp.float32)
                for frame in range(frames):
                    state = state_halo[side, frame].astype(jnp.float32)
                    state = state + growth[frame] * arrived
                    spread(wide_states, place, frame, state.astype(jnp.bfloat16))

            @pl.when(jnp.logical_not(has_before))
            def _():
                for frame in range(frames):
                    spread(wide_states, place, frame, state_halo[side, frame])

    def product(i, low, high):
        window = [wide_states[i + tap] for tap in range(low, high)]
        window = window[0] if high == low + 1 else jnp.concatenate(window, axis=-1)
        flat = window.reshape(frames * width, (high - low) * 3 * channels)
        taps = wout[low * 3 * channels : high * 3 * channels]
        value = jnp.dot(flat, taps, preferred_element_type=jnp.float32)
        return value.reshape(frames, width, channels)

    def write(i, value):
        for frame in range(frames):
            updated = lat[frame, i].astype(jnp.float32) + jax.nn.gelu(value[frame])
            result[frame, i] = updated.astype(jnp.bfloat16)
        pltpu.make_async_copy(result.at[:, i], out_hbm.at[:, i], store_sem.at[i]).start()

    def close(side, exists):
        i, place, low = (0, 0, 0) if side == 0 else (strip - 1, strip + 1, 2)
        outer(place, side, exists)

        @pl.when(exists)
        def _():
            write(i, mixed[side] + product(i, low, low + 1))

        @pl.when(jnp.logical_not(exists))
        def _():
            write(i, mixed[side])

    middle = list(range(1, strip - 1))
    bottom = strip - 1

    load_lat.wait()
    for i in range(strip):
        for frame in range(frames):
            spread(wide, i + 1, frame, lat[frame, i])
    load_win.wait()

    def drive_top():
        border(0, 0, has_up)
        drive(0)
        settle(0, 1, has_up)

    def drive_bottom():
        border(strip + 1, 1, has_down)
        drive(bottom)
        settle(bottom, 0, has_down)

    def by_parity(one, two):
        @pl.when(even)
        def _():
            one()

        @pl.when(jnp.logical_not(even))
        def _():
            two()

    for i in middle[:1]:
        drive(i)
    by_parity(drive_bottom, drive_top)
    by_parity(drive_top, drive_bottom)
    for i in middle[1:]:
        drive(i)

    @pl.when(has_before)
    def _():
        for i in middle[:1]:
            advance(i)
        for i in middle[:1]:
            stretch(i)

        def low_first():
            advance(bottom, 0, has_down)
            advance(0, 1, has_up)

        def high_first():
            advance(0, 1, has_up)
            advance(bottom, 0, has_down)

        by_parity(low_first, high_first)

    load_wout.wait()

    @pl.when(jnp.logical_not(has_before))
    def _():
        for i in middle[:1]:
            stretch(i)

    stretch(0)
    stretch(bottom)
    mixed[0] = product(0, 1, 3)

    @pl.when(has_before)
    def _():
        for i in middle[1:]:
            advance(i)

    for i in middle[1:]:
        stretch(i)
    mixed[1] = product(bottom, 0, 2)
    for i in middle:
        write(i, product(i, 0, 3))

    def top_last():
        close(1, has_down)
        close(0, has_up)

    def bottom_last():
        close(0, has_up)
        close(1, has_down)

    by_parity(top_last, bottom_last)

    @pl.when(has_down)
    def _():
        halo_copy(0).wait_send()
        state_copy(0).wait_send()

    @pl.when(has_up)
    def _():
        halo_copy(1).wait_send()
        state_copy(1).wait_send()

    @pl.when(jnp.logical_and(has_down, has_before))
    def _():
        for piece in range(PIECES):
            relay_copy(0, piece).wait_send()

    @pl.when(jnp.logical_and(has_up, has_before))
    def _():
        for piece in range(PIECES):
            relay_copy(1, piece).wait_send()

    @pl.when(has_after)
    def _():
        for i in range(strip):
            for piece in range(PIECES):
                carry_copy(i, piece).wait_send()

    for i in range(strip):
        pltpu.make_async_copy(result.at[:, i], out_hbm.at[:, i], store_sem.at[i]).wait()


def local(positions, strips, latents, weight_in, weight_out, decay_table, decay_index):
    frames, strip, width, channels = latents.shape
    link = jnp.bfloat16 if positions <= 8 else jnp.float32
    half = jnp.bfloat16
    dma = pltpu.SemaphoreType.DMA
    anywhere = pl.BlockSpec(memory_space=pl.ANY)
    return pl.pallas_call(
        functools.partial(kernel, positions, strips),
        out_shape=jax.ShapeDtypeStruct(latents.shape, latents.dtype),
        in_specs=[
            anywhere,
            anywhere,
            anywhere,
            pl.BlockSpec(memory_space=pltpu.SMEM),
            pl.BlockSpec(memory_space=pltpu.VMEM),
        ],
        out_specs=anywhere,
        scratch_shapes=[
            pltpu.VMEM((frames, strip, width, channels), half),
            pltpu.VMEM((9 * channels, channels), half),
            pltpu.VMEM((9 * channels, channels), half),
            pltpu.VMEM((2, frames, width, channels), half),
            pltpu.VMEM((strip + 2, frames, width, 3 * channels), half),
            pltpu.VMEM((strip, frames, width, channels), jnp.float32),
            pltpu.VMEM((strip, width, channels), link),
            pltpu.VMEM((strip, width, channels), link),
            pltpu.VMEM((strip, frames, width, channels), half),
            pltpu.VMEM((2, frames, width, channels), half),
            pltpu.VMEM((2, width, channels), link),
            pltpu.VMEM((2, frames, width, channels), jnp.float32),
            pltpu.VMEM((strip + 2, frames, width, 3 * channels), half),
            pltpu.VMEM((frames, strip, width, channels), half),
            dma((3,)),
            dma((strip,)),
            dma((2,)),
            dma((2,)),
            dma((2,)),
            dma((2,)),
            dma((strip, PIECES)),
            dma((strip, PIECES)),
            dma((2, PIECES)),
            dma((2, PIECES)),
        ],
        compiler_params=pltpu.CompilerParams(collective_id=0, has_side_effects=True),
    )(
        latents,
        weight_in.reshape(9 * channels, channels),
        weight_out.reshape(9 * channels, channels),
        decay_table,
        decay_index.reshape(1, channels),
    )


def solution(mesh):
    in_specs = (P(("groups", "tm"), "rows", None, None), P(), P(), P(), P())
    out_specs = P(("groups", "tm"), "rows", None, None)
    body = functools.partial(local, mesh.shape["tm"], mesh.shape["rows"])
    return jax.shard_map(body, mesh=mesh, in_specs=in_specs, out_specs=out_specs, check_vma=False)
```

```python
import functools

import jax
import jax.numpy as jnp
from jax import lax
from jax.experimental import pallas as pl
from jax.experimental.pallas import tpu as pltpu
from jax.sharding import PartitionSpec as P

MESH = pl.DeviceIdType.MESH
PIECES = 4


def kernel(
    positions,
    strips,
    lat_hbm,
    win_hbm,
    wout_hbm,
    table_hbm,
    index_hbm,
    out_hbm,
    lat,
    win,
    wout,
    halo,
    wide,
    partial,
    carry,
    passed,
    rounded,
    state_halo,
    relayed,
    mixed,
    table_ref,
    index_ref,
    wide_states,
    result,
    load_sem,
    store_sem,
    halo_send,
    halo_recv,
    state_send,
    state_recv,
    carry_send,
    carry_recv,
    relay_send,
    relay_recv,
):
    frames, strip, width, channels = lat.shape
    row = lax.axis_index("rows")
    moment = lax.axis_index("tm")
    has_up, has_down = row > 0, row < strips - 1
    has_before, has_after = moment > 0, moment < positions - 1
    span = width // PIECES

    load_lat = pltpu.make_async_copy(lat_hbm, lat, load_sem.at[0])
    load_win = pltpu.make_async_copy(win_hbm, win, load_sem.at[1])
    load_wout = pltpu.make_async_copy(wout_hbm, wout, load_sem.at[2])
    load_table = pltpu.make_async_copy(table_hbm, table_ref, load_sem.at[3])
    load_index = pltpu.make_async_copy(index_hbm, index_ref, load_sem.at[4])

    barrier = pltpu.get_barrier_semaphore()
    near = (
        (has_up, {"rows": row - 1}),
        (has_down, {"rows": row + 1}),
        (has_before, {"tm": moment - 1}),
        (has_after, {"tm": moment + 1}),
    )
    total = 0
    for exists, where in near:
        total = total + exists.astype(jnp.int32)

        @pl.when(exists)
        def _():
            pl.semaphore_signal(barrier, inc=1, device_id=where, device_id_type=MESH)

    load_lat.start()
    load_table.start()
    load_index.start()
    load_win.start()
    load_wout.start()
    pl.semaphore_wait(barrier, total)

    def halo_copy(side):
        source = lat_hbm.at[:, strip - 1] if side == 0 else lat_hbm.at[:, 0]
        target = row + 1 if side == 0 else row - 1
        return pltpu.make_async_remote_copy(
            src_ref=source,
            dst_ref=halo.at[side],
            send_sem=halo_send.at[side],
            recv_sem=halo_recv.at[side],
            device_id={"rows": target},
            device_id_type=MESH,
        )

    def state_copy(side):
        source = rounded.at[strip - 1] if side == 0 else rounded.at[0]
        target = row + 1 if side == 0 else row - 1
        return pltpu.make_async_remote_copy(
            src_ref=source,
            dst_ref=state_halo.at[side],
            send_sem=state_send.at[side],
            recv_sem=state_recv.at[side],
            device_id={"rows": target},
            device_id_type=MESH,
        )

    def relay_copy(side, piece):
        part = pl.ds(piece * span, span)
        edge = strip - 1 if side == 0 else 0
        target = row + 1 if side == 0 else row - 1
        return pltpu.make_async_remote_copy(
            src_ref=carry.at[edge, part],
            dst_ref=relayed.at[side, part],
            send_sem=relay_send.at[side, piece],
            recv_sem=relay_recv.at[side, piece],
            device_id={"rows": target},
            device_id_type=MESH,
        )

    def carry_copy(i, piece):
        part = pl.ds(piece * span, span)
        return pltpu.make_async_remote_copy(
            src_ref=passed.at[i, part],
            dst_ref=carry.at[i, part],
            send_sem=carry_send.at[i, piece],
            recv_sem=carry_recv.at[i, piece],
            device_id={"tm": moment + 1},
            device_id_type=MESH,
        )

    even = lax.rem(row, 2) == 0

    @pl.when(jnp.logical_and(has_up, even))
    def _():
        halo_copy(1).start()

    @pl.when(has_down)
    def _():
        halo_copy(0).start()

    @pl.when(jnp.logical_and(has_up, jnp.logical_not(even)))
    def _():
        halo_copy(1).start()

    load_table.wait()
    load_index.wait()
    chosen = index_ref[...]
    decays = jnp.zeros(chosen.shape, jnp.float32)
    for level in range(table_ref.shape[0]):
        decays = jnp.where(chosen == level, table_ref[level], decays)
    growth = [decays]
    for _ in range(frames - 1):
        growth.append(growth[-1] * decays)

    column = lax.broadcasted_iota(jnp.int32, (width, channels), 0)

    def spread(target, place, frame, value):
        full = value.astype(jnp.float32)
        before = jnp.where(column == 0, 0.0, pltpu.roll(full, 1, 0))
        after = jnp.where(column == width - 1, 0.0, pltpu.roll(full, width - 1, 0))
        target[place, frame, :, 0:channels] = before.astype(jnp.bfloat16)
        target[place, frame, :, channels : 2 * channels] = value
        target[place, frame, :, 2 * channels : 3 * channels] = after.astype(jnp.bfloat16)

    def border(i, side, exists):
        @pl.when(exists)
        def _():
            halo_copy(side).wait_recv()
            for frame in range(frames):
                spread(wide, i, frame, halo[side, frame])

        @pl.when(jnp.logical_not(exists))
        def _():
            wide[i] = jnp.zeros(wide.shape[1:], wide.dtype)

    def drive(i):
        window = jnp.concatenate([wide[i], wide[i + 1], wide[i + 2]], axis=-1)
        flat = window.reshape(frames * width, 9 * channels)
        driven = jnp.dot(flat, win[...], preferred_element_type=jnp.float32).reshape(
            frames, width, channels
        )
        running = driven[0]
        partial[i, 0] = running
        for frame in range(1, frames):
            running = decays * running + driven[frame]
            partial[i, frame] = running

        @pl.when(jnp.logical_not(has_before))
        def _():
            passed[i] = partial[i, frames - 1].astype(passed.dtype)

            @pl.when(has_after)
            def _():
                for piece in range(PIECES):
                    carry_copy(i, piece).start()

    def settle(i, side, exists):
        for frame in range(frames):
            rounded[i, frame] = partial[i, frame].astype(jnp.bfloat16)

        @pl.when(exists)
        def _():
            state_copy(side).start()

    def advance(i, side=None, exists=None):
        for piece in range(PIECES):
            part = pl.ds(piece * span, span)
            carry_copy(i, piece).wait_recv()
            if side is not None:

                @pl.when(exists)
                def _():
                    relay_copy(side, piece).start()

            arrived = carry[i, part].astype(jnp.float32)
            last = partial[i, frames - 1, part] + growth[frames - 1] * arrived
            passed[i, part] = last.astype(passed.dtype)

            @pl.when(has_after)
            def _():
                carry_copy(i, piece).start()

            partial[i, frames - 1, part] = last
            for frame in range(frames - 1):
                partial[i, frame, part] = partial[i, frame, part] + growth[frame] * arrived

    def stretch(i):
        for frame in range(frames):
            spread(wide_states, i + 1, frame, partial[i, frame].astype(jnp.bfloat16))

    def outer(place, side, exists):
        @pl.when(exists)
        def _():
            state_copy(side).wait_recv()

            @pl.when(has_before)
            def _():
                for piece in range(PIECES):
                    relay_copy(side, piece).wait_recv()
                arrived = relayed[side].astype(jnp.float32)
                for frame in range(frames):
                    state = state_halo[side, frame].astype(jnp.float32)
                    state = state + growth[frame] * arrived
                    spread(wide_states, place, frame, state.astype(jnp.bfloat16))

            @pl.when(jnp.logical_not(has_before))
            def _():
                for frame in range(frames):
                    spread(wide_states, place, frame, state_halo[side, frame])

    def product(i, low, high):
        window = [wide_states[i + tap] for tap in range(low, high)]
        window = window[0] if high == low + 1 else jnp.concatenate(window, axis=-1)
        flat = window.reshape(frames * width, (high - low) * 3 * channels)
        taps = wout[low * 3 * channels : high * 3 * channels]
        value = jnp.dot(flat, taps, preferred_element_type=jnp.float32)
        return value.reshape(frames, width, channels)

    def write(i, value):
        for frame in range(frames):
            updated = lat[frame, i].astype(jnp.float32) + jax.nn.gelu(value[frame])
            result[frame, i] = updated.astype(jnp.bfloat16)
        pltpu.make_async_copy(result.at[:, i], out_hbm.at[:, i], store_sem.at[i]).start()

    def close(side, exists):
        i, place, low = (0, 0, 0) if side == 0 else (strip - 1, strip + 1, 2)
        outer(place, side, exists)

        @pl.when(exists)
        def _():
            write(i, mixed[side] + product(i, low, low + 1))

        @pl.when(jnp.logical_not(exists))
        def _():
            write(i, mixed[side])

    middle = list(range(1, strip - 1))
    bottom = strip - 1

    load_lat.wait()
    for i in range(strip):
        for frame in range(frames):
            spread(wide, i + 1, frame, lat[frame, i])
    load_win.wait()

    def drive_top():
        border(0, 0, has_up)
        drive(0)
        settle(0, 1, has_up)

    def drive_bottom():
        border(strip + 1, 1, has_down)
        drive(bottom)
        settle(bottom, 0, has_down)

    def by_parity(one, two):
        @pl.when(even)
        def _():
            one()

        @pl.when(jnp.logical_not(even))
        def _():
            two()

    for i in middle[:1]:
        drive(i)
    by_parity(drive_bottom, drive_top)
    by_parity(drive_top, drive_bottom)
    for i in middle[1:]:
        drive(i)

    @pl.when(has_before)
    def _():
        for i in middle[:1]:
            advance(i)
        for i in middle[:1]:
            stretch(i)

        def low_first():
            advance(bottom, 0, has_down)
            advance(0, 1, has_up)

        def high_first():
            advance(0, 1, has_up)
            advance(bottom, 0, has_down)

        by_parity(low_first, high_first)

    load_wout.wait()

    @pl.when(jnp.logical_not(has_before))
    def _():
        for i in middle[:1]:
            stretch(i)

    stretch(0)
    stretch(bottom)
    mixed[0] = product(0, 1, 3)

    @pl.when(has_before)
    def _():
        for i in middle[1:]:
            advance(i)

    for i in middle[1:]:
        stretch(i)
    mixed[1] = product(bottom, 0, 2)
    for i in middle:
        write(i, product(i, 0, 3))

    def top_last():
        close(1, has_down)
        close(0, has_up)

    def bottom_last():
        close(0, has_up)
        close(1, has_down)

    by_parity(top_last, bottom_last)

    @pl.when(has_down)
    def _():
        halo_copy(0).wait_send()
        state_copy(0).wait_send()

    @pl.when(has_up)
    def _():
        halo_copy(1).wait_send()
        state_copy(1).wait_send()

    @pl.when(jnp.logical_and(has_down, has_before))
    def _():
        for piece in range(PIECES):
            relay_copy(0, piece).wait_send()

    @pl.when(jnp.logical_and(has_up, has_before))
    def _():
        for piece in range(PIECES):
            relay_copy(1, piece).wait_send()

    @pl.when(has_after)
    def _():
        for i in range(strip):
            for piece in range(PIECES):
                carry_copy(i, piece).wait_send()

    for i in range(strip):
        pltpu.make_async_copy(result.at[:, i], out_hbm.at[:, i], store_sem.at[i]).wait()


def local(positions, strips, latents, weight_in, weight_out, decay_table, decay_index):
    frames, strip, width, channels = latents.shape
    link = jnp.bfloat16 if positions <= 8 else jnp.float32
    half = jnp.bfloat16
    dma = pltpu.SemaphoreType.DMA
    anywhere = pl.BlockSpec(memory_space=pl.ANY)
    return pl.pallas_call(
        functools.partial(kernel, positions, strips),
        out_shape=jax.ShapeDtypeStruct(latents.shape, latents.dtype),
        in_specs=[
            anywhere,
            anywhere,
            anywhere,
            anywhere,
            anywhere,
        ],
        out_specs=anywhere,
        scratch_shapes=[
            pltpu.VMEM((frames, strip, width, channels), half),
            pltpu.VMEM((9 * channels, channels), half),
            pltpu.VMEM((9 * channels, channels), half),
            pltpu.VMEM((2, frames, width, channels), half),
            pltpu.VMEM((strip + 2, frames, width, 3 * channels), half),
            pltpu.VMEM((strip, frames, width, channels), jnp.float32),
            pltpu.VMEM((strip, width, channels), link),
            pltpu.VMEM((strip, width, channels), link),
            pltpu.VMEM((strip, frames, width, channels), half),
            pltpu.VMEM((2, frames, width, channels), half),
            pltpu.VMEM((2, width, channels), link),
            pltpu.VMEM((2, frames, width, channels), jnp.float32),
            pltpu.SMEM(decay_table.shape, jnp.float32),
            pltpu.VMEM((1, channels), jnp.int32),
            pltpu.VMEM((strip + 2, frames, width, 3 * channels), half),
            pltpu.VMEM((frames, strip, width, channels), half),
            dma((5,)),
            dma((strip,)),
            dma((2,)),
            dma((2,)),
            dma((2,)),
            dma((2,)),
            dma((strip, PIECES)),
            dma((strip, PIECES)),
            dma((2, PIECES)),
            dma((2, PIECES)),
        ],
        compiler_params=pltpu.CompilerParams(collective_id=0, has_side_effects=True, vmem_limit_bytes=32 * 1024 * 1024),
    )(
        pltpu.with_memory_space_constraint(latents, pltpu.HBM),
        pltpu.with_memory_space_constraint(weight_in.reshape(9 * channels, channels), pltpu.HBM),
        pltpu.with_memory_space_constraint(weight_out.reshape(9 * channels, channels), pltpu.HBM),
        pltpu.with_memory_space_constraint(decay_table, pltpu.HBM),
        pltpu.with_memory_space_constraint(decay_index.reshape(1, channels), pltpu.HBM),
    )


def solution(mesh):
    in_specs = (P(("groups", "tm"), "rows", None, None), P(), P(), P(), P())
    out_specs = P(("groups", "tm"), "rows", None, None)
    body = functools.partial(local, mesh.shape["tm"], mesh.shape["rows"])
    return jax.shard_map(body, mesh=mesh, in_specs=in_specs, out_specs=out_specs, check_vma=False)
```

```python
import functools

import jax
import jax.numpy as jnp
from jax import lax
from jax.experimental import pallas as pl
from jax.experimental.pallas import tpu as pltpu
from jax.sharding import PartitionSpec as P

MESH = pl.DeviceIdType.MESH
PIECES = 4


def kernel(
    positions,
    strips,
    lat_hbm,
    win_hbm,
    wout_hbm,
    table_hbm,
    index_hbm,
    out_hbm,
    lat,
    win,
    wout,
    halo,
    wide,
    partial,
    carry,
    passed,
    rounded,
    state_halo,
    relayed,
    mixed,
    table_ref,
    index_ref,
    wide_states,
    result,
    load_sem,
    store_sem,
    halo_send,
    halo_recv,
    state_send,
    state_recv,
    carry_send,
    carry_recv,
    relay_send,
    relay_recv,
):
    frames, strip, width, channels = lat.shape
    row = lax.axis_index("rows")
    moment = lax.axis_index("tm")
    has_up, has_down = row > 0, row < strips - 1
    has_before, has_after = moment > 0, moment < positions - 1
    span = width // PIECES

    load_lat = pltpu.make_async_copy(lat_hbm, lat, load_sem.at[0])
    load_win = pltpu.make_async_copy(win_hbm, win, load_sem.at[1])
    load_wout = pltpu.make_async_copy(wout_hbm, wout, load_sem.at[2])
    load_table = pltpu.make_async_copy(table_hbm, table_ref, load_sem.at[3])
    load_index = pltpu.make_async_copy(index_hbm, index_ref, load_sem.at[4])

    barrier = pltpu.get_barrier_semaphore()
    near = (
        (has_up, {"rows": row - 1}),
        (has_down, {"rows": row + 1}),
        (has_before, {"tm": moment - 1}),
        (has_after, {"tm": moment + 1}),
    )
    total = 0
    for exists, where in near:
        total = total + exists.astype(jnp.int32)

        @pl.when(exists)
        def _():
            pl.semaphore_signal(barrier, inc=1, device_id=where, device_id_type=MESH)

    load_lat.start()
    load_table.start()
    load_index.start()
    load_win.start()
    load_wout.start()
    pl.semaphore_wait(barrier, total)

    def halo_copy(side):
        source = lat_hbm.at[:, strip - 1] if side == 0 else lat_hbm.at[:, 0]
        target = row + 1 if side == 0 else row - 1
        return pltpu.make_async_remote_copy(
            src_ref=source,
            dst_ref=halo.at[side],
            send_sem=halo_send.at[side],
            recv_sem=halo_recv.at[side],
            device_id={"rows": target},
            device_id_type=MESH,
        )

    def state_copy(side):
        source = rounded.at[strip - 1] if side == 0 else rounded.at[0]
        target = row + 1 if side == 0 else row - 1
        return pltpu.make_async_remote_copy(
            src_ref=source,
            dst_ref=state_halo.at[side],
            send_sem=state_send.at[side],
            recv_sem=state_recv.at[side],
            device_id={"rows": target},
            device_id_type=MESH,
        )

    def relay_copy(side, piece):
        part = pl.ds(piece * span, span)
        edge = strip - 1 if side == 0 else 0
        target = row + 1 if side == 0 else row - 1
        return pltpu.make_async_remote_copy(
            src_ref=carry.at[edge, part],
            dst_ref=relayed.at[side, part],
            send_sem=relay_send.at[side, piece],
            recv_sem=relay_recv.at[side, piece],
            device_id={"rows": target},
            device_id_type=MESH,
        )

    def carry_copy(i, piece):
        part = pl.ds(piece * span, span)
        return pltpu.make_async_remote_copy(
            src_ref=passed.at[i, part],
            dst_ref=carry.at[i, part],
            send_sem=carry_send.at[i, piece],
            recv_sem=carry_recv.at[i, piece],
            device_id={"tm": moment + 1},
            device_id_type=MESH,
        )

    even = lax.rem(row, 2) == 0

    @pl.when(jnp.logical_and(has_up, even))
    def _():
        halo_copy(1).start()

    @pl.when(has_down)
    def _():
        halo_copy(0).start()

    @pl.when(jnp.logical_and(has_up, jnp.logical_not(even)))
    def _():
        halo_copy(1).start()

    load_table.wait()
    load_index.wait()
    chosen = index_ref[...]
    decays = jnp.zeros(chosen.shape, jnp.float32)
    for level in range(table_ref.shape[0]):
        decays = jnp.where(chosen == level, table_ref[level], decays)
    growth = [decays]
    for _ in range(frames - 1):
        growth.append(growth[-1] * decays)

    column = lax.broadcasted_iota(jnp.int32, (width, channels), 0)

    def spread(target, place, frame, value):
        full = value.astype(jnp.float32)
        before = jnp.where(column == 0, 0.0, pltpu.roll(full, 1, 0))
        after = jnp.where(column == width - 1, 0.0, pltpu.roll(full, width - 1, 0))
        target[place, frame, :, 0:channels] = before.astype(jnp.bfloat16)
        target[place, frame, :, channels : 2 * channels] = value
        target[place, frame, :, 2 * channels : 3 * channels] = after.astype(jnp.bfloat16)

    def border(i, side, exists):
        @pl.when(exists)
        def _():
            halo_copy(side).wait_recv()
            for frame in range(frames):
                spread(wide, i, frame, halo[side, frame])

        @pl.when(jnp.logical_not(exists))
        def _():
            wide[i] = jnp.zeros(wide.shape[1:], wide.dtype)

    def drive(i):
        window = jnp.concatenate([wide[i], wide[i + 1], wide[i + 2]], axis=-1)
        flat = window.reshape(frames * width, 9 * channels)
        driven = jnp.dot(flat, win[...], preferred_element_type=jnp.float32).reshape(
            frames, width, channels
        )
        running = driven[0]
        partial[i, 0] = running
        for frame in range(1, frames):
            running = decays * running + driven[frame]
            partial[i, frame] = running

    def begin(i):
        @pl.when(jnp.logical_not(has_before))
        def _():
            passed[i] = partial[i, frames - 1].astype(passed.dtype)

            @pl.when(has_after)
            def _():
                for piece in range(PIECES):
                    carry_copy(i, piece).start()

    def settle(i, side, exists):
        begin(i)
        for frame in range(frames):
            rounded[i, frame] = partial[i, frame].astype(jnp.bfloat16)

        @pl.when(exists)
        def _():
            state_copy(side).start()

    def advance(i, side=None, exists=None):
        for piece in range(PIECES):
            part = pl.ds(piece * span, span)
            carry_copy(i, piece).wait_recv()
            if side is not None:

                @pl.when(exists)
                def _():
                    relay_copy(side, piece).start()

            arrived = carry[i, part].astype(jnp.float32)
            last = partial[i, frames - 1, part] + growth[frames - 1] * arrived
            passed[i, part] = last.astype(passed.dtype)

            @pl.when(has_after)
            def _():
                carry_copy(i, piece).start()

            partial[i, frames - 1, part] = last
            for frame in range(frames - 1):
                partial[i, frame, part] = partial[i, frame, part] + growth[frame] * arrived

    def stretch(i):
        for frame in range(frames):
            spread(wide_states, i + 1, frame, partial[i, frame].astype(jnp.bfloat16))

    def outer(place, side, exists):
        @pl.when(exists)
        def _():
            state_copy(side).wait_recv()

            @pl.when(has_before)
            def _():
                for piece in range(PIECES):
                    relay_copy(side, piece).wait_recv()
                arrived = relayed[side].astype(jnp.float32)
                for frame in range(frames):
                    state = state_halo[side, frame].astype(jnp.float32)
                    state = state + growth[frame] * arrived
                    spread(wide_states, place, frame, state.astype(jnp.bfloat16))

            @pl.when(jnp.logical_not(has_before))
            def _():
                for frame in range(frames):
                    spread(wide_states, place, frame, state_halo[side, frame])

    def product(i, taps):
        window = [wide_states[i + tap] for tap in taps]
        window = window[0] if len(taps) == 1 else jnp.concatenate(window, axis=-1)
        flat = window.reshape(frames * width, len(taps) * 3 * channels)
        depth = 3 * channels
        rows = [wout[tap * depth : (tap + 1) * depth] for tap in taps]
        rows = rows[0] if len(taps) == 1 else jnp.concatenate(rows, axis=0)
        value = jnp.dot(flat, rows, preferred_element_type=jnp.float32)
        return value.reshape(frames, width, channels)

    def write(i, value):
        for frame in range(frames):
            updated = lat[frame, i].astype(jnp.float32) + jax.nn.gelu(value[frame])
            result[frame, i] = updated.astype(jnp.bfloat16)
        pltpu.make_async_copy(result.at[:, i], out_hbm.at[:, i], store_sem.at[i]).start()

    def close(side, exists):
        i, place, low = (0, 0, 0) if side == 0 else (strip - 1, strip + 1, 2)
        outer(place, side, exists)

        @pl.when(exists)
        def _():
            write(i, mixed[i] + product(i, [low]))

        @pl.when(jnp.logical_not(exists))
        def _():
            write(i, mixed[i])

    middle = list(range(1, strip - 1))
    bottom = strip - 1

    load_lat.wait()
    for i in range(strip):
        for frame in range(frames):
            spread(wide, i + 1, frame, lat[frame, i])
    load_win.wait()

    def drive_top():
        border(0, 0, has_up)
        drive(0)
        settle(0, 1, has_up)

    def drive_bottom():
        border(strip + 1, 1, has_down)
        drive(bottom)
        settle(bottom, 0, has_down)

    def by_parity(one, two):
        @pl.when(even)
        def _():
            one()

        @pl.when(jnp.logical_not(even))
        def _():
            two()

    late = middle[1:]
    early = moment == 1

    for i in middle[:1]:
        drive(i)
        begin(i)
    by_parity(drive_bottom, drive_top)
    for i in late:
        drive(i)

    @pl.when(early)
    def _():
        for i in middle[:1]:
            advance(i)

    by_parity(drive_top, drive_bottom)
    for i in late:
        begin(i)

    @pl.when(jnp.logical_and(has_before, jnp.logical_not(early)))
    def _():
        for i in middle[:1]:
            advance(i)

    @pl.when(has_before)
    def _():
        def low_first():
            advance(bottom, 0, has_down)
            advance(0, 1, has_up)

        def high_first():
            advance(0, 1, has_up)
            advance(bottom, 0, has_down)

        by_parity(low_first, high_first)

    @pl.when(jnp.logical_and(has_before, has_after))
    def _():
        for i in late:
            advance(i)

    load_wout.wait()
    ready = [i for i in range(strip) if i not in late]
    for i in ready:
        stretch(i)
    for i in range(strip):
        taps = [tap for tap in range(3) if i + tap - 1 in ready]
        mixed[i] = product(i, taps) if taps else jnp.zeros(mixed.shape[1:], jnp.float32)

    @pl.when(jnp.logical_and(has_before, jnp.logical_not(has_after)))
    def _():
        for i in late:
            advance(i)

    for i in late:
        stretch(i)
    for i in range(strip):
        taps = [tap for tap in range(3) if i + tap - 1 in late]
        if i in middle:
            write(i, mixed[i] + product(i, taps) if taps else mixed[i])
        elif taps:
            mixed[i] = mixed[i] + product(i, taps)

    def top_last():
        close(1, has_down)
        close(0, has_up)

    def bottom_last():
        close(0, has_up)
        close(1, has_down)

    by_parity(top_last, bottom_last)

    @pl.when(has_down)
    def _():
        halo_copy(0).wait_send()
        state_copy(0).wait_send()

    @pl.when(has_up)
    def _():
        halo_copy(1).wait_send()
        state_copy(1).wait_send()

    @pl.when(jnp.logical_and(has_down, has_before))
    def _():
        for piece in range(PIECES):
            relay_copy(0, piece).wait_send()

    @pl.when(jnp.logical_and(has_up, has_before))
    def _():
        for piece in range(PIECES):
            relay_copy(1, piece).wait_send()

    @pl.when(has_after)
    def _():
        for i in range(strip):
            for piece in range(PIECES):
                carry_copy(i, piece).wait_send()

    for i in range(strip):
        pltpu.make_async_copy(result.at[:, i], out_hbm.at[:, i], store_sem.at[i]).wait()


def local(positions, strips, latents, weight_in, weight_out, decay_table, decay_index):
    frames, strip, width, channels = latents.shape
    link = jnp.bfloat16 if positions <= 8 else jnp.float32
    half = jnp.bfloat16
    dma = pltpu.SemaphoreType.DMA
    anywhere = pl.BlockSpec(memory_space=pl.ANY)
    return pl.pallas_call(
        functools.partial(kernel, positions, strips),
        out_shape=jax.ShapeDtypeStruct(latents.shape, latents.dtype),
        in_specs=[
            anywhere,
            anywhere,
            anywhere,
            anywhere,
            anywhere,
        ],
        out_specs=anywhere,
        scratch_shapes=[
            pltpu.VMEM((frames, strip, width, channels), half),
            pltpu.VMEM((9 * channels, channels), half),
            pltpu.VMEM((9 * channels, channels), half),
            pltpu.VMEM((2, frames, width, channels), half),
            pltpu.VMEM((strip + 2, frames, width, 3 * channels), half),
            pltpu.VMEM((strip, frames, width, channels), jnp.float32),
            pltpu.VMEM((strip, width, channels), link),
            pltpu.VMEM((strip, width, channels), link),
            pltpu.VMEM((strip, frames, width, channels), half),
            pltpu.VMEM((2, frames, width, channels), half),
            pltpu.VMEM((2, width, channels), link),
            pltpu.VMEM((strip, frames, width, channels), jnp.float32),
            pltpu.SMEM(decay_table.shape, jnp.float32),
            pltpu.VMEM((1, channels), jnp.int32),
            pltpu.VMEM((strip + 2, frames, width, 3 * channels), half),
            pltpu.VMEM((frames, strip, width, channels), half),
            dma((5,)),
            dma((strip,)),
            dma((2,)),
            dma((2,)),
            dma((2,)),
            dma((2,)),
            dma((strip, PIECES)),
            dma((strip, PIECES)),
            dma((2, PIECES)),
            dma((2, PIECES)),
        ],
        compiler_params=pltpu.CompilerParams(collective_id=0, has_side_effects=True, vmem_limit_bytes=32 * 1024 * 1024),
    )(
        pltpu.with_memory_space_constraint(latents, pltpu.HBM),
        pltpu.with_memory_space_constraint(weight_in.reshape(9 * channels, channels), pltpu.HBM),
        pltpu.with_memory_space_constraint(weight_out.reshape(9 * channels, channels), pltpu.HBM),
        pltpu.with_memory_space_constraint(decay_table, pltpu.HBM),
        pltpu.with_memory_space_constraint(decay_index.reshape(1, channels), pltpu.HBM),
    )


def solution(mesh):
    in_specs = (P(("groups", "tm"), "rows", None, None), P(), P(), P(), P())
    out_specs = P(("groups", "tm"), "rows", None, None)
    body = functools.partial(local, mesh.shape["tm"], mesh.shape["rows"])
    return jax.shard_map(body, mesh=mesh, in_specs=in_specs, out_specs=out_specs, check_vma=False)
```

```python
import functools

import jax
import jax.numpy as jnp
from jax import lax
from jax.experimental import pallas as pl
from jax.experimental.pallas import tpu as pltpu
from jax.sharding import PartitionSpec as P

MESH = pl.DeviceIdType.MESH
PIECES = 8


def kernel(
    positions,
    strips,
    lat_hbm,
    win_hbm,
    wout_hbm,
    table_hbm,
    index_hbm,
    out_hbm,
    lat,
    win,
    wout,
    halo,
    wide,
    partial,
    carry,
    passed,
    rounded,
    state_halo,
    relayed,
    mixed,
    table_ref,
    index_ref,
    wide_states,
    result,
    load_sem,
    store_sem,
    halo_send,
    halo_recv,
    state_send,
    state_recv,
    carry_send,
    carry_recv,
    relay_send,
    relay_recv,
):
    frames, strip, width, channels = lat.shape
    row = lax.axis_index("rows")
    moment = lax.axis_index("tm")
    has_up, has_down = row > 0, row < strips - 1
    has_before, has_after = moment > 0, moment < positions - 1
    span = width // PIECES

    load_lat = pltpu.make_async_copy(lat_hbm, lat, load_sem.at[0])
    load_win = pltpu.make_async_copy(win_hbm, win, load_sem.at[1])
    load_wout = pltpu.make_async_copy(wout_hbm, wout, load_sem.at[2])
    load_table = pltpu.make_async_copy(table_hbm, table_ref, load_sem.at[3])
    load_index = pltpu.make_async_copy(index_hbm, index_ref, load_sem.at[4])

    barrier = pltpu.get_barrier_semaphore()
    near = (
        (has_up, {"rows": row - 1}),
        (has_down, {"rows": row + 1}),
        (has_before, {"tm": moment - 1}),
        (has_after, {"tm": moment + 1}),
    )
    total = 0
    for exists, where in near:
        total = total + exists.astype(jnp.int32)

        @pl.when(exists)
        def _():
            pl.semaphore_signal(barrier, inc=1, device_id=where, device_id_type=MESH)

    load_lat.start()
    load_table.start()
    load_index.start()
    load_win.start()
    load_wout.start()
    pl.semaphore_wait(barrier, total)

    def halo_copy(side):
        source = lat_hbm.at[:, strip - 1] if side == 0 else lat_hbm.at[:, 0]
        target = row + 1 if side == 0 else row - 1
        return pltpu.make_async_remote_copy(
            src_ref=source,
            dst_ref=halo.at[side],
            send_sem=halo_send.at[side],
            recv_sem=halo_recv.at[side],
            device_id={"rows": target},
            device_id_type=MESH,
        )

    def state_copy(side):
        source = rounded.at[strip - 1] if side == 0 else rounded.at[0]
        target = row + 1 if side == 0 else row - 1
        return pltpu.make_async_remote_copy(
            src_ref=source,
            dst_ref=state_halo.at[side],
            send_sem=state_send.at[side],
            recv_sem=state_recv.at[side],
            device_id={"rows": target},
            device_id_type=MESH,
        )

    def relay_copy(side, piece):
        part = pl.ds(piece * span, span)
        edge = strip - 1 if side == 0 else 0
        target = row + 1 if side == 0 else row - 1
        return pltpu.make_async_remote_copy(
            src_ref=carry.at[edge, part],
            dst_ref=relayed.at[side, part],
            send_sem=relay_send.at[side, piece],
            recv_sem=relay_recv.at[side, piece],
            device_id={"rows": target},
            device_id_type=MESH,
        )

    def carry_copy(i, piece):
        part = pl.ds(piece * span, span)
        return pltpu.make_async_remote_copy(
            src_ref=passed.at[i, part],
            dst_ref=carry.at[i, part],
            send_sem=carry_send.at[i, piece],
            recv_sem=carry_recv.at[i, piece],
            device_id={"tm": moment + 1},
            device_id_type=MESH,
        )

    even = lax.rem(row, 2) == 0

    @pl.when(jnp.logical_and(has_up, even))
    def _():
        halo_copy(1).start()

    @pl.when(has_down)
    def _():
        halo_copy(0).start()

    @pl.when(jnp.logical_and(has_up, jnp.logical_not(even)))
    def _():
        halo_copy(1).start()

    load_table.wait()
    load_index.wait()
    chosen = index_ref[...]
    decays = jnp.zeros(chosen.shape, jnp.float32)
    for level in range(table_ref.shape[0]):
        decays = jnp.where(chosen == level, table_ref[level], decays)
    growth = [decays]
    for _ in range(frames - 1):
        growth.append(growth[-1] * decays)

    column = lax.broadcasted_iota(jnp.int32, (width, channels), 0)

    def spread(target, place, frame, value):
        full = value.astype(jnp.float32)
        before = jnp.where(column == 0, 0.0, pltpu.roll(full, 1, 0))
        after = jnp.where(column == width - 1, 0.0, pltpu.roll(full, width - 1, 0))
        target[place, frame, :, 0:channels] = before.astype(jnp.bfloat16)
        target[place, frame, :, channels : 2 * channels] = value
        target[place, frame, :, 2 * channels : 3 * channels] = after.astype(jnp.bfloat16)

    def border(i, side, exists):
        @pl.when(exists)
        def _():
            halo_copy(side).wait_recv()
            for frame in range(frames):
                spread(wide, i, frame, halo[side, frame])

        @pl.when(jnp.logical_not(exists))
        def _():
            wide[i] = jnp.zeros(wide.shape[1:], wide.dtype)

    def drive(i):
        window = jnp.concatenate([wide[i], wide[i + 1], wide[i + 2]], axis=-1)
        flat = window.reshape(frames * width, 9 * channels)
        driven = jnp.dot(flat, win[...], preferred_element_type=jnp.float32).reshape(
            frames, width, channels
        )
        running = driven[0]
        partial[i, 0] = running
        for frame in range(1, frames):
            running = decays * running + driven[frame]
            partial[i, frame] = running

    def begin(i):
        @pl.when(jnp.logical_not(has_before))
        def _():
            passed[i] = partial[i, frames - 1].astype(passed.dtype)

            @pl.when(has_after)
            def _():
                for piece in range(PIECES):
                    carry_copy(i, piece).start()

    def settle(i, side, exists):
        begin(i)
        for frame in range(frames):
            rounded[i, frame] = partial[i, frame].astype(jnp.bfloat16)

        @pl.when(exists)
        def _():
            state_copy(side).start()

    def advance(i, side=None, exists=None):
        for piece in range(PIECES):
            part = pl.ds(piece * span, span)
            carry_copy(i, piece).wait_recv()
            if side is not None:

                @pl.when(exists)
                def _():
                    relay_copy(side, piece).start()

            arrived = carry[i, part].astype(jnp.float32)
            last = partial[i, frames - 1, part] + growth[frames - 1] * arrived
            passed[i, part] = last.astype(passed.dtype)

            @pl.when(has_after)
            def _():
                carry_copy(i, piece).start()

            partial[i, frames - 1, part] = last
            for frame in range(frames - 1):
                partial[i, frame, part] = partial[i, frame, part] + growth[frame] * arrived

    def stretch(i):
        for frame in range(frames):
            spread(wide_states, i + 1, frame, partial[i, frame].astype(jnp.bfloat16))

    def outer(place, side, exists):
        @pl.when(exists)
        def _():
            state_copy(side).wait_recv()

            @pl.when(has_before)
            def _():
                for piece in range(PIECES):
                    relay_copy(side, piece).wait_recv()
                arrived = relayed[side].astype(jnp.float32)
                for frame in range(frames):
                    state = state_halo[side, frame].astype(jnp.float32)
                    state = state + growth[frame] * arrived
                    spread(wide_states, place, frame, state.astype(jnp.bfloat16))

            @pl.when(jnp.logical_not(has_before))
            def _():
                for frame in range(frames):
                    spread(wide_states, place, frame, state_halo[side, frame])

    def product(i, taps):
        window = [wide_states[i + tap] for tap in taps]
        window = window[0] if len(taps) == 1 else jnp.concatenate(window, axis=-1)
        flat = window.reshape(frames * width, len(taps) * 3 * channels)
        depth = 3 * channels
        rows = [wout[tap * depth : (tap + 1) * depth] for tap in taps]
        rows = rows[0] if len(taps) == 1 else jnp.concatenate(rows, axis=0)
        value = jnp.dot(flat, rows, preferred_element_type=jnp.float32)
        return value.reshape(frames, width, channels)

    def write(i, value):
        for frame in range(frames):
            updated = lat[frame, i].astype(jnp.float32) + jax.nn.gelu(value[frame])
            result[frame, i] = updated.astype(jnp.bfloat16)
        pltpu.make_async_copy(result.at[:, i], out_hbm.at[:, i], store_sem.at[i]).start()

    def close(side, exists):
        i, place, low = (0, 0, 0) if side == 0 else (strip - 1, strip + 1, 2)
        outer(place, side, exists)

        @pl.when(exists)
        def _():
            write(i, mixed[i] + product(i, [low]))

        @pl.when(jnp.logical_not(exists))
        def _():
            write(i, mixed[i])

    middle = list(range(1, strip - 1))
    bottom = strip - 1

    load_lat.wait()
    for i in range(strip):
        for frame in range(frames):
            spread(wide, i + 1, frame, lat[frame, i])
    load_win.wait()

    def drive_top():
        border(0, 0, has_up)
        drive(0)
        settle(0, 1, has_up)

    def drive_bottom():
        border(strip + 1, 1, has_down)
        drive(bottom)
        settle(bottom, 0, has_down)

    def by_parity(one, two):
        @pl.when(even)
        def _():
            one()

        @pl.when(jnp.logical_not(even))
        def _():
            two()

    late = middle[1:]
    early = moment == 1

    for i in middle[:1]:
        drive(i)
        begin(i)
    by_parity(drive_bottom, drive_top)
    for i in late:
        drive(i)

    @pl.when(early)
    def _():
        for i in middle[:1]:
            advance(i)

    by_parity(drive_top, drive_bottom)
    for i in late:
        begin(i)

    @pl.when(jnp.logical_and(has_before, jnp.logical_not(early)))
    def _():
        for i in middle[:1]:
            advance(i)

    @pl.when(has_before)
    def _():
        def low_first():
            advance(bottom, 0, has_down)
            advance(0, 1, has_up)

        def high_first():
            advance(0, 1, has_up)
            advance(bottom, 0, has_down)

        by_parity(low_first, high_first)

    @pl.when(jnp.logical_and(has_before, has_after))
    def _():
        for i in late:
            advance(i)

    load_wout.wait()
    ready = [i for i in range(strip) if i not in late]
    for i in ready:
        stretch(i)
    for i in range(strip):
        taps = [tap for tap in range(3) if i + tap - 1 in ready]
        mixed[i] = product(i, taps) if taps else jnp.zeros(mixed.shape[1:], jnp.float32)

    @pl.when(jnp.logical_and(has_before, jnp.logical_not(has_after)))
    def _():
        for i in late:
            advance(i)

    for i in late:
        stretch(i)
    for i in range(strip):
        taps = [tap for tap in range(3) if i + tap - 1 in late]
        if i in middle:
            write(i, mixed[i] + product(i, taps) if taps else mixed[i])
        elif taps:
            mixed[i] = mixed[i] + product(i, taps)

    def top_last():
        close(1, has_down)
        close(0, has_up)

    def bottom_last():
        close(0, has_up)
        close(1, has_down)

    by_parity(top_last, bottom_last)

    @pl.when(has_down)
    def _():
        halo_copy(0).wait_send()
        state_copy(0).wait_send()

    @pl.when(has_up)
    def _():
        halo_copy(1).wait_send()
        state_copy(1).wait_send()

    @pl.when(jnp.logical_and(has_down, has_before))
    def _():
        for piece in range(PIECES):
            relay_copy(0, piece).wait_send()

    @pl.when(jnp.logical_and(has_up, has_before))
    def _():
        for piece in range(PIECES):
            relay_copy(1, piece).wait_send()

    @pl.when(has_after)
    def _():
        for i in range(strip):
            for piece in range(PIECES):
                carry_copy(i, piece).wait_send()

    for i in range(strip):
        pltpu.make_async_copy(result.at[:, i], out_hbm.at[:, i], store_sem.at[i]).wait()


def local(positions, strips, latents, weight_in, weight_out, decay_table, decay_index):
    frames, strip, width, channels = latents.shape
    link = jnp.bfloat16 if positions <= 8 else jnp.float32
    half = jnp.bfloat16
    dma = pltpu.SemaphoreType.DMA
    anywhere = pl.BlockSpec(memory_space=pl.ANY)
    return pl.pallas_call(
        functools.partial(kernel, positions, strips),
        out_shape=jax.ShapeDtypeStruct(latents.shape, latents.dtype),
        in_specs=[
            anywhere,
            anywhere,
            anywhere,
            anywhere,
            anywhere,
        ],
        out_specs=anywhere,
        scratch_shapes=[
            pltpu.VMEM((frames, strip, width, channels), half),
            pltpu.VMEM((9 * channels, channels), half),
            pltpu.VMEM((9 * channels, channels), half),
            pltpu.VMEM((2, frames, width, channels), half),
            pltpu.VMEM((strip + 2, frames, width, 3 * channels), half),
            pltpu.VMEM((strip, frames, width, channels), jnp.float32),
            pltpu.VMEM((strip, width, channels), link),
            pltpu.VMEM((strip, width, channels), link),
            pltpu.VMEM((strip, frames, width, channels), half),
            pltpu.VMEM((2, frames, width, channels), half),
            pltpu.VMEM((2, width, channels), link),
            pltpu.VMEM((strip, frames, width, channels), jnp.float32),
            pltpu.SMEM(decay_table.shape, jnp.float32),
            pltpu.VMEM((1, channels), jnp.int32),
            pltpu.VMEM((strip + 2, frames, width, 3 * channels), half),
            pltpu.VMEM((frames, strip, width, channels), half),
            dma((5,)),
            dma((strip,)),
            dma((2,)),
            dma((2,)),
            dma((2,)),
            dma((2,)),
            dma((strip, PIECES)),
            dma((strip, PIECES)),
            dma((2, PIECES)),
            dma((2, PIECES)),
        ],
        compiler_params=pltpu.CompilerParams(collective_id=0, has_side_effects=True, vmem_limit_bytes=32 * 1024 * 1024),
    )(
        pltpu.with_memory_space_constraint(latents, pltpu.HBM),
        pltpu.with_memory_space_constraint(weight_in.reshape(9 * channels, channels), pltpu.HBM),
        pltpu.with_memory_space_constraint(weight_out.reshape(9 * channels, channels), pltpu.HBM),
        pltpu.with_memory_space_constraint(decay_table, pltpu.HBM),
        pltpu.with_memory_space_constraint(decay_index.reshape(1, channels), pltpu.HBM),
    )


def solution(mesh):
    in_specs = (P(("groups", "tm"), "rows", None, None), P(), P(), P(), P())
    out_specs = P(("groups", "tm"), "rows", None, None)
    body = functools.partial(local, mesh.shape["tm"], mesh.shape["rows"])
    return jax.shard_map(body, mesh=mesh, in_specs=in_specs, out_specs=out_specs, check_vma=False)
```
